256 devices in a mesh: dp: 32 (over x, z), fsdp: 8 (over y, core).
Axes of the slice: x: 4, y: 4, z: 8, core: 2. Of those that a mesh axis runs over, the one named last changes fastest.
Arguments:
- hidden: bfloat16 [8192, 28672], P('dp', 'fsdp'), may hold values from -6 to 6
- cotangent: bfloat16 [8192, 8192], P('dp', 'fsdp'), may hold values from -6 to 6
- region_ids: int32 [8192], P('dp'), may hold values from 0 to 255, as said below
- adapter_a: bfloat16 [256, 64, 28672], P('dp', None, 'fsdp'), may hold values from -0.03125 to 0.03125
- adapter_b: bfloat16 [256, 64, 8192], P('dp', None, 'fsdp'), may hold values from -0.75 to 0.75
Outputs:
- grad_a: bfloat16 [256, 64, 28672], P('dp', None, 'fsdp')
- grad_b: bfloat16 [256, 64, 8192], P('dp', None, 'fsdp')
- grad_hidden: bfloat16 [8192, 28672], P('dp', 'fsdp')
The draws below stay inside these ranges and needn't reach their ends.
Inputs may be any that keep to these rules, and one draw needn't show every extreme that they name: `region_ids`: region r belongs to owner r // 8. In each aligned block of 256 tokens (the tokens of one index of dp) the ids never fall, and at most 24 tokens name regions of one owner; in every block 4 owners, the same ones in every block, reach that bound.
All inputs are finite; a program needn't handle non-finite values.
Results may differ from the reference program's by a relative error of at most 0.0049.
Values may be sent and summed in bfloat16 or wider, within the bound.
A program may use at most 128 MiB of HBM per device.

```python
import jax
import jax.numpy as jnp
from jax import lax

D = 8192
FF = 28672
RANK = 64
ADAPT_DEV = 8
TOK_G = 256
ADAPTERS = 256
TOKENS = 8192
CAPACITY = 24
N_DP = 32


def draw_region_ids(key, part):
    owners = N_DP
    blocks = N_DP
    hotter = owners // 8
    colder = owners - hotter
    remain = TOK_G - hotter * CAPACITY
    base_count = remain // colder
    extra_count = remain % colder
    ranking = jnp.arange(owners, dtype=jnp.int32)
    cold_rank = ranking - hotter
    drawn = jnp.where(ranking < hotter, CAPACITY, base_count + (cold_rank < extra_count).astype(jnp.int32))
    pairs = max(colder // 2, 1)
    half_base = base_count // 2
    shifts = jax.random.randint(jax.random.fold_in(key, 2), (blocks, pairs), -half_base, half_base + 1)
    pair_index = jnp.clip(cold_rank // 2, 0, pairs - 1)
    sign_value = 1 - 2 * (cold_rank % 2)
    usable = (cold_rank >= 0) & (cold_rank // 2 < colder // 2)
    shift_full = jnp.where(usable[None, :], sign_value[None, :] * shifts[:, pair_index], 0)
    counts_rank = drawn[None, :] + shift_full
    order = jax.random.permutation(jax.random.fold_in(key, 1), owners)
    rank_of = jnp.argsort(order)
    counts_owner = jnp.take(counts_rank, rank_of, axis=1)
    ends = jnp.cumsum(counts_owner, axis=1)
    position = jnp.arange(TOK_G, dtype=jnp.int32)
    owner_of = jnp.sum((position[None, :, None] >= ends[:, None, :]).astype(jnp.int32), axis=2)
    local_pick = jax.random.randint(jax.random.fold_in(key, 3), (blocks, TOK_G), 0, ADAPT_DEV)
    regions = jnp.sort(owner_of * ADAPT_DEV + local_pick, axis=1)
    return regions.reshape(-1).astype(jnp.int32)


def level_of(stream_key, shape, cuts, least, largest):
    level = 1.0
    for dim, shards_of in cuts:
        draws = jax.random.uniform(jax.random.fold_in(jax.random.fold_in(stream_key, 6), dim), (shards_of,), jnp.float32, least / len(cuts), largest / len(cuts))
        level = level * jnp.repeat(jnp.exp(draws), shape[dim] // shards_of).reshape((-1,) + (1,) * (len(shape) - 1 - dim))
    return level


def noise(stream_key, extent, width, reach, cuts=(), kind=jnp.bfloat16):
    gain = level_of(stream_key, extent, cuts, -0.22, 0.18) if cuts else 1.0
    result = jax.random.normal(stream_key, extent, jnp.float32) * width * gain
    return jnp.minimum(jnp.maximum(result, -reach), reach).astype(kind)


def setup_inputs(seed: int = 0) -> dict:
    arg_keys = jax.random.split(jax.random.key(seed), 6)
    return {
        "hidden": noise(arg_keys[0], (TOKENS, FF), 1.0, 6.0, ((0, 32), (1, 8))),
        "cotangent": noise(arg_keys[1], (TOKENS, D), 1.0, 6.0, ((0, 32), (1, 8))),
        "region_ids": draw_region_ids(jax.random.fold_in(arg_keys[5], 71), 0),
        "adapter_a": noise(arg_keys[3], (ADAPTERS, RANK, FF), FF ** -0.5, 0.03125, ((0, 32), (2, 8))),
        "adapter_b": noise(arg_keys[4], (ADAPTERS, RANK, D), RANK ** -0.5, 0.75, ((0, 32), (2, 8))),
    }


def reference(hidden, cotangent, region_ids, adapter_a, adapter_b):
    block = 16
    count = TOKENS // block
    hidden_blocks = hidden.reshape(count, block, FF)
    cotangent_blocks = cotangent.reshape(count, block, D)
    region_blocks = region_ids.reshape(count, block)

    def advance(carry, inputs):
        total_a, total_b = carry
        hidden_part, cotangent_part, region_part = inputs
        chosen_a = adapter_a[region_part].astype(jnp.float32)
        chosen_b = adapter_b[region_part].astype(jnp.float32)
        hidden_float = hidden_part.astype(jnp.float32)
        cotangent_float = cotangent_part.astype(jnp.float32)
        project = jnp.einsum("tf,taf->ta", hidden_float, chosen_a).astype(jnp.bfloat16)
        back = jnp.einsum("td,tad->ta", cotangent_float, chosen_b).astype(jnp.bfloat16)
        project_float = project.astype(jnp.float32)
        back_float = back.astype(jnp.float32)
        returned = jnp.einsum("ta,taf->tf", back_float, chosen_a).astype(jnp.bfloat16)
        total_a = total_a.at[region_part].add(jnp.einsum("ta,tf->taf", back_float, hidden_float))
        total_b = total_b.at[region_part].add(jnp.einsum("ta,td->tad", project_float, cotangent_float))
        return (total_a, total_b), returned

    start = (jnp.zeros((ADAPTERS, RANK, FF), jnp.float32), jnp.zeros((ADAPTERS, RANK, D), jnp.float32))
    (total_a, total_b), returned = lax.scan(advance, start, (hidden_blocks, cotangent_blocks, region_blocks))
    return total_a.astype(jnp.bfloat16), total_b.astype(jnp.bfloat16), returned.reshape(TOKENS, FF)
```

```python
import jax
import jax.numpy as jnp
from jax import lax
from jax.sharding import PartitionSpec as P


def contract_rows(left, right):
    return lax.dot_general(
        left, right, (((0,), (0,)), ((), ())), preferred_element_type=jnp.float32
    )


def contract_cols(left, right):
    return lax.dot_general(
        left, right, (((1,), (1,)), ((), ())), preferred_element_type=jnp.float32
    )


def shards(hidden, cotangent, region_ids, adapter_a, adapter_b):
    owner_count = lax.axis_size("dp")
    token_count = hidden.shape[0]
    local_count = adapter_a.shape[0]
    rank_width = adapter_a.shape[1]
    hidden_width = hidden.shape[1]
    model_width = cotangent.shape[1]
    capacity = 3 * token_count // owner_count
    owner_of = region_ids // local_count
    owner_ids = jnp.arange(owner_count, dtype=jnp.int32)
    counts = jnp.sum((owner_of[:, None] == owner_ids[None, :]).astype(jnp.int32), axis=0)
    starts = jnp.cumsum(counts) - counts
    slot_index = jnp.arange(capacity, dtype=jnp.int32)
    usable = slot_index[None, :] < counts[:, None]
    row_index = jnp.where(usable, starts[:, None] + slot_index[None, :], 0)
    id_width = 128
    send_local = jnp.where(usable, region_ids[row_index] % local_count, local_count).astype(
        jnp.bfloat16
    )
    send = jnp.concatenate(
        [
            hidden[row_index],
            cotangent[row_index],
            jnp.broadcast_to(send_local[:, :, None], (owner_count, capacity, id_width)),
        ],
        axis=-1,
    )
    recv = lax.all_to_all(send, "dp", split_axis=0, concat_axis=0, tiled=True)
    total_rows = owner_count * capacity
    recv = recv.reshape(total_rows, hidden_width + model_width + id_width)
    got_hidden = recv[:, :hidden_width]
    got_cotangent = recv[:, hidden_width : hidden_width + model_width]
    got_local = recv[:, hidden_width + model_width]
    local_ids = jnp.arange(local_count).astype(jnp.bfloat16)
    onehot = (got_local[:, None] == local_ids[None, :]).astype(jnp.float32)
    flat_a = adapter_a.reshape(local_count * rank_width, hidden_width)
    flat_b = adapter_b.reshape(local_count * rank_width, model_width)
    part_down = contract_cols(got_hidden, flat_a).reshape(total_rows, local_count, rank_width)
    part_back = contract_cols(got_cotangent, flat_b).reshape(total_rows, local_count, rank_width)
    pick_down = jnp.sum(part_down * onehot[:, :, None], axis=1)
    pick_back = jnp.sum(part_back * onehot[:, :, None], axis=1)
    full = lax.psum(jnp.concatenate([pick_down, pick_back], axis=1), "fsdp")
    full_down = full[:, :rank_width].astype(jnp.bfloat16)
    full_back = full[:, rank_width:].astype(jnp.bfloat16)
    mask = onehot.astype(jnp.bfloat16)[:, :, None]
    down_rows = (mask * full_down[:, None, :]).reshape(total_rows, local_count * rank_width)
    back_rows = (mask * full_back[:, None, :]).reshape(total_rows, local_count * rank_width)
    grad_b = (
        contract_rows(down_rows, got_cotangent)
        .reshape(local_count, rank_width, model_width)
        .astype(jnp.bfloat16)
    )
    grad_a = (
        contract_rows(back_rows, got_hidden)
        .reshape(local_count, rank_width, hidden_width)
        .astype(jnp.bfloat16)
    )
    returned = jnp.dot(back_rows, flat_a, preferred_element_type=jnp.float32).astype(jnp.bfloat16)
    returned = returned.reshape(owner_count, capacity, hidden_width)
    arrived = lax.all_to_all(returned, "dp", split_axis=0, concat_axis=0, tiled=True)
    before = jnp.sum((owner_of[None, :] < owner_of[:, None]).astype(jnp.int32), axis=1)
    position = jnp.arange(token_count, dtype=jnp.int32) - before
    grad_hidden = arrived.reshape(total_rows, hidden_width)[owner_of * capacity + position]
    return (grad_a, grad_b, grad_hidden)


def solution(mesh):
    return jax.shard_map(
        shards,
        mesh=mesh,
        in_specs=(
            P("dp", "fsdp"),
            P("dp", "fsdp"),
            P("dp"),
            P("dp", None, "fsdp"),
            P("dp", None, "fsdp"),
        ),
        out_specs=(P("dp", None, "fsdp"), P("dp", None, "fsdp"), P("dp", "fsdp")),
        check_vma=False,
    )
```

```python
import jax
import jax.numpy as jnp
from jax import lax
from jax.sharding import PartitionSpec as P


def contract_rows(left, right):
    return lax.dot_general(
        left, right, (((0,), (0,)), ((), ())), preferred_element_type=jnp.float32
    )


def contract_cols(left, right):
    return lax.dot_general(
        left, right, (((1,), (1,)), ((), ())), preferred_element_type=jnp.float32
    )


def shards(hidden, cotangent, region_ids, adapter_a, adapter_b):
    owner_count = lax.axis_size("dp")
    token_count = hidden.shape[0]
    local_count = adapter_a.shape[0]
    rank_width = adapter_a.shape[1]
    hidden_width = hidden.shape[1]
    model_width = cotangent.shape[1]
    capacity = 3 * token_count // owner_count
    owner_of = region_ids // local_count
    owner_ids = jnp.arange(owner_count, dtype=jnp.int32)
    counts = jnp.sum((owner_of[:, None] == owner_ids[None, :]).astype(jnp.int32), axis=0)
    starts = jnp.cumsum(counts) - counts
    slot_index = jnp.arange(capacity, dtype=jnp.int32)
    usable = slot_index[None, :] < counts[:, None]
    row_index = jnp.where(usable, starts[:, None] + slot_index[None, :], token_count)
    id_width = 128
    table = jnp.concatenate(
        [
            hidden,
            cotangent,
            jnp.broadcast_to(
                (region_ids % local_count).astype(jnp.bfloat16)[:, None], (token_count, id_width)
            ),
        ],
        axis=-1,
    )
    flat_a = adapter_a.reshape(local_count * rank_width, hidden_width)
    flat_b = adapter_b.reshape(local_count * rank_width, model_width)
    local_ids = jnp.arange(local_count).astype(jnp.bfloat16)
    pieces = 2
    piece = capacity // pieces
    grad_a = None
    grad_b = None
    arrived = []
    for k in range(pieces):
        send = table.at[row_index[:, k * piece : (k + 1) * piece]].get(
            mode="fill", fill_value=local_count
        )
        recv = lax.all_to_all(send, "dp", split_axis=0, concat_axis=0, tiled=True)
        if k > 0:
            recv, full = lax.optimization_barrier((recv, full))
        rows = owner_count * piece
        recv = recv.reshape(rows, hidden_width + model_width + id_width)
        got_hidden = recv[:, :hidden_width]
        got_cotangent = recv[:, hidden_width : hidden_width + model_width]
        got_local = recv[:, hidden_width + model_width]
        onehot = (got_local[:, None] == local_ids[None, :]).astype(jnp.float32)
        part_down = contract_cols(got_hidden, flat_a).reshape(rows, local_count, rank_width)
        part_back = contract_cols(got_cotangent, flat_b).reshape(rows, local_count, rank_width)
        pick_down = jnp.sum(part_down * onehot[:, :, None], axis=1)
        pick_back = jnp.sum(part_back * onehot[:, :, None], axis=1)
        full = lax.psum(jnp.concatenate([pick_down, pick_back], axis=1), "fsdp")
        full_down = full[:, :rank_width].astype(jnp.bfloat16)
        full_back = full[:, rank_width:].astype(jnp.bfloat16)
        mask = onehot.astype(jnp.bfloat16)[:, :, None]
        down_rows = (mask * full_down[:, None, :]).reshape(rows, local_count * rank_width)
        back_rows = (mask * full_back[:, None, :]).reshape(rows, local_count * rank_width)
        returned = jnp.dot(back_rows, flat_a, preferred_element_type=jnp.float32).astype(
            jnp.bfloat16
        )
        returned = returned.reshape(owner_count, piece, hidden_width)
        arrived.append(lax.all_to_all(returned, "dp", split_axis=0, concat_axis=0, tiled=True))
        part_b = contract_rows(down_rows, got_cotangent)
        part_a = contract_rows(back_rows, got_hidden)
        grad_b = part_b if grad_b is None else grad_b + part_b
        grad_a = part_a if grad_a is None else grad_a + part_a
    grad_b = grad_b.reshape(local_count, rank_width, model_width).astype(jnp.bfloat16)
    grad_a = grad_a.reshape(local_count, rank_width, hidden_width).astype(jnp.bfloat16)
    arrived = jnp.concatenate(arrived, axis=1)
    before = jnp.sum((owner_of[None, :] < owner_of[:, None]).astype(jnp.int32), axis=1)
    position = jnp.arange(token_count, dtype=jnp.int32) - before
    grad_hidden = arrived.reshape(owner_count * capacity, hidden_width)[
        owner_of * capacity + position
    ]
    return (grad_a, grad_b, grad_hidden)


def solution(mesh):
    return jax.shard_map(
        shards,
        mesh=mesh,
        in_specs=(
            P("dp", "fsdp"),
            P("dp", "fsdp"),
            P("dp"),
            P("dp", None, "fsdp"),
            P("dp", None, "fsdp"),
        ),
        out_specs=(P("dp", None, "fsdp"), P("dp", None, "fsdp"), P("dp", "fsdp")),
        check_vma=False,
    )
```

```python
import jax
import jax.numpy as jnp
from jax import lax
from jax.sharding import PartitionSpec as P


def contract_rows(left, right):
    return lax.dot_general(
        left, right, (((0,), (0,)), ((), ())), preferred_element_type=jnp.float32
    )


def contract_cols(left, right):
    return lax.dot_general(
        left, right, (((1,), (1,)), ((), ())), preferred_element_type=jnp.float32
    )


def shards(hidden, cotangent, region_ids, adapter_a, adapter_b):
    owner_count = lax.axis_size("dp")
    token_count = hidden.shape[0]
    local_count = adapter_a.shape[0]
    rank_width = adapter_a.shape[1]
    hidden_width = hidden.shape[1]
    model_width = cotangent.shape[1]
    capacity = 3 * token_count // owner_count
    owner_of = region_ids // local_count
    owner_ids = jnp.arange(owner_count, dtype=jnp.int32)
    counts = jnp.sum((owner_of[:, None] == owner_ids[None, :]).astype(jnp.int32), axis=0)
    starts = jnp.cumsum(counts) - counts
    slot_index = jnp.arange(capacity, dtype=jnp.int32)
    usable = slot_index[None, :] < counts[:, None]
    total_rows = owner_count * capacity
    token_index = jnp.arange(token_count, dtype=jnp.int32)
    wanted = jnp.where(usable, starts[:, None] + slot_index[None, :], -1).reshape(total_rows)
    pick = (wanted[:, None] == token_index[None, :]).astype(jnp.bfloat16)
    id_width = 128
    table = jnp.concatenate(
        [
            hidden,
            cotangent,
            jnp.broadcast_to(
                (region_ids % local_count + 1).astype(jnp.bfloat16)[:, None],
                (token_count, id_width),
            ),
        ],
        axis=-1,
    )
    send = jnp.dot(pick, table, preferred_element_type=jnp.float32).astype(jnp.bfloat16)
    send = send.reshape(owner_count, capacity, hidden_width + model_width + id_width)
    recv = lax.all_to_all(send, "dp", split_axis=0, concat_axis=0, tiled=True)
    recv = recv.reshape(total_rows, hidden_width + model_width + id_width)
    got_hidden = recv[:, :hidden_width]
    got_cotangent = recv[:, hidden_width : hidden_width + model_width]
    got_local = recv[:, hidden_width + model_width] - 1
    local_ids = jnp.arange(local_count).astype(jnp.bfloat16)
    onehot = (got_local[:, None] == local_ids[None, :]).astype(jnp.float32)
    flat_a = adapter_a.reshape(local_count * rank_width, hidden_width)
    flat_b = adapter_b.reshape(local_count * rank_width, model_width)
    part_down = contract_cols(got_hidden, flat_a).reshape(total_rows, local_count, rank_width)
    part_back = contract_cols(got_cotangent, flat_b).reshape(total_rows, local_count, rank_width)
    pick_down = jnp.sum(part_down * onehot[:, :, None], axis=1)
    pick_back = jnp.sum(part_back * onehot[:, :, None], axis=1)
    full = lax.psum(jnp.concatenate([pick_down, pick_back], axis=1), "fsdp")
    full_down = full[:, :rank_width].astype(jnp.bfloat16)
    full_back = full[:, rank_width:].astype(jnp.bfloat16)
    mask = onehot.astype(jnp.bfloat16)[:, :, None]
    down_rows = (mask * full_down[:, None, :]).reshape(total_rows, local_count * rank_width)
    back_rows = (mask * full_back[:, None, :]).reshape(total_rows, local_count * rank_width)
    grad_b = (
        contract_rows(down_rows, got_cotangent)
        .reshape(local_count, rank_width, model_width)
        .astype(jnp.bfloat16)
    )
    grad_a = (
        contract_rows(back_rows, got_hidden)
        .reshape(local_count, rank_width, hidden_width)
        .astype(jnp.bfloat16)
    )
    returned = jnp.dot(back_rows, flat_a, preferred_element_type=jnp.float32).astype(jnp.bfloat16)
    returned = returned.reshape(owner_count, capacity, hidden_width)
    arrived = lax.all_to_all(returned, "dp", split_axis=0, concat_axis=0, tiled=True)
    before = jnp.sum((owner_of[None, :] < owner_of[:, None]).astype(jnp.int32), axis=1)
    source = owner_of * capacity + token_index - before
    slot_all = jnp.arange(total_rows, dtype=jnp.int32)
    place = (source[:, None] == slot_all[None, :]).astype(jnp.bfloat16)
    grad_hidden = jnp.dot(
        place, arrived.reshape(total_rows, hidden_width), preferred_element_type=jnp.float32
    ).astype(jnp.bfloat16)
    return (grad_a, grad_b, grad_hidden)


def solution(mesh):
    return jax.shard_map(
        shards,
        mesh=mesh,
        in_specs=(
            P("dp", "fsdp"),
            P("dp", "fsdp"),
            P("dp"),
            P("dp", None, "fsdp"),
            P("dp", None, "fsdp"),
        ),
        out_specs=(P("dp", None, "fsdp"), P("dp", None, "fsdp"), P("dp", "fsdp")),
        check_vma=False,
    )
```

```python
import jax
import jax.numpy as jnp
from jax import lax
from jax.sharding import PartitionSpec as P


def contract_rows(left, right):
    return lax.dot_general(
        left, right, (((0,), (0,)), ((), ())), preferred_element_type=jnp.float32
    )


def contract_cols(left, right):
    return lax.dot_general(
        left, right, (((1,), (1,)), ((), ())), preferred_element_type=jnp.float32
    )


def fsdp_sum(x):
    n = lax.axis_size("fsdp")
    if n & (n - 1):
        return lax.psum(x, "fsdp")
    step = 1
    while step < n:
        x = x + lax.ppermute(x, "fsdp", [(i, i ^ step) for i in range(n)])
        step *= 2
    return x


def shards(hidden, cotangent, region_ids, adapter_a, adapter_b):
    owner_count = lax.axis_size("dp")
    token_count = hidden.shape[0]
    local_count = adapter_a.shape[0]
    rank_width = adapter_a.shape[1]
    hidden_width = hidden.shape[1]
    model_width = cotangent.shape[1]
    capacity = 3 * token_count // owner_count
    owner_of = region_ids // local_count
    owner_ids = jnp.arange(owner_count, dtype=jnp.int32)
    counts = jnp.sum((owner_of[:, None] == owner_ids[None, :]).astype(jnp.int32), axis=0)
    starts = jnp.cumsum(counts) - counts
    slot_index = jnp.arange(capacity, dtype=jnp.int32)
    usable = slot_index[None, :] < counts[:, None]
    total_rows = owner_count * capacity
    token_index = jnp.arange(token_count, dtype=jnp.int32)
    wanted = jnp.where(usable, starts[:, None] + slot_index[None, :], -1).reshape(total_rows)
    pick = (wanted[:, None] == token_index[None, :]).astype(jnp.bfloat16)
    table = jnp.concatenate([hidden, cotangent], axis=-1)
    send = jnp.dot(pick, table, preferred_element_type=jnp.float32).astype(jnp.bfloat16)
    send = send.reshape(owner_count, capacity, hidden_width + model_width)
    recv = lax.all_to_all(send, "dp", split_axis=0, concat_axis=0, tiled=True)
    recv = recv.reshape(total_rows, hidden_width + model_width)
    got_hidden = recv[:, :hidden_width]
    got_cotangent = recv[:, hidden_width:]
    me = lax.axis_index("dp")
    all_ids = lax.all_gather(region_ids, "dp")
    all_owner = all_ids // local_count
    in_counts = jnp.sum((all_owner == me).astype(jnp.int32), axis=1)
    in_starts = jnp.sum((all_owner < me).astype(jnp.int32), axis=1)
    hit = token_index[None, None, :] == (in_starts[:, None] + slot_index[None, :])[:, :, None]
    slot_region = jnp.sum(jnp.where(hit, all_ids[:, None, :] % local_count, 0), axis=2)
    valid = slot_index[None, :] < in_counts[:, None]
    got_local = jnp.where(valid, slot_region, -1).reshape(total_rows)
    local_ids = jnp.arange(local_count, dtype=jnp.int32)
    onehot = (got_local[:, None] == local_ids[None, :]).astype(jnp.float32)
    flat_a = adapter_a.reshape(local_count * rank_width, hidden_width)
    flat_b = adapter_b.reshape(local_count * rank_width, model_width)
    part_down = contract_cols(got_hidden, flat_a).reshape(total_rows, local_count, rank_width)
    part_back = contract_cols(got_cotangent, flat_b).reshape(total_rows, local_count, rank_width)
    pick_down = jnp.sum(part_down * onehot[:, :, None], axis=1)
    pick_back = jnp.sum(part_back * onehot[:, :, None], axis=1)
    full = fsdp_sum(jnp.concatenate([pick_down, pick_back], axis=1))
    full_down = full[:, :rank_width].astype(jnp.bfloat16)
    full_back = full[:, rank_width:].astype(jnp.bfloat16)
    mask = onehot.astype(jnp.bfloat16)[:, :, None]
    down_rows = (mask * full_down[:, None, :]).reshape(total_rows, local_count * rank_width)
    back_rows = (mask * full_back[:, None, :]).reshape(total_rows, local_count * rank_width)
    grad_b = (
        contract_rows(down_rows, got_cotangent)
        .reshape(local_count, rank_width, model_width)
        .astype(jnp.bfloat16)
    )
    grad_a = (
        contract_rows(back_rows, got_hidden)
        .reshape(local_count, rank_width, hidden_width)
        .astype(jnp.bfloat16)
    )
    returned = jnp.dot(back_rows, flat_a, preferred_element_type=jnp.float32).astype(jnp.bfloat16)
    returned = returned.reshape(owner_count, capacity, hidden_width)
    arrived = lax.all_to_all(returned, "dp", split_axis=0, concat_axis=0, tiled=True)
    before = jnp.sum((owner_of[None, :] < owner_of[:, None]).astype(jnp.int32), axis=1)
    source = owner_of * capacity + token_index - before
    slot_all = jnp.arange(total_rows, dtype=jnp.int32)
    place = (source[:, None] == slot_all[None, :]).astype(jnp.bfloat16)
    grad_hidden = jnp.dot(
        place, arrived.reshape(total_rows, hidden_width), preferred_element_type=jnp.float32
    ).astype(jnp.bfloat16)
    return (grad_a, grad_b, grad_hidden)


def solution(mesh):
    return jax.shard_map(
        shards,
        mesh=mesh,
        in_specs=(
            P("dp", "fsdp"),
            P("dp", "fsdp"),
            P("dp"),
            P("dp", None, "fsdp"),
            P("dp", None, "fsdp"),
        ),
        out_specs=(P("dp", None, "fsdp"), P("dp", None, "fsdp"), P("dp", "fsdp")),
        check_vma=False,
    )
```

```python
import jax
import jax.numpy as jnp
from jax import lax
from jax.sharding import PartitionSpec as P


def contract_rows(left, right):
    return lax.dot_general(
        left, right, (((0,), (0,)), ((), ())), preferred_element_type=jnp.float32
    )


def contract_cols(left, right):
    return lax.dot_general(
        left, right, (((1,), (1,)), ((), ())), preferred_element_type=jnp.float32
    )


def fsdp_sum(x):
    n = lax.axis_size("fsdp")
    if n & (n - 1):
        return lax.psum(x, "fsdp")
    step = 1
    while step < n:
        x = x + lax.ppermute(x, "fsdp", [(i, i ^ step) for i in range(n)])
        step *= 2
    return x


def shards(hidden, cotangent, region_ids, adapter_a, adapter_b):
    owner_count = lax.axis_size("dp")
    token_count = hidden.shape[0]
    local_count = adapter_a.shape[0]
    rank_width = adapter_a.shape[1]
    hidden_width = hidden.shape[1]
    model_width = cotangent.shape[1]
    capacity = 3 * token_count // owner_count
    owner_of = region_ids // local_count
    owner_ids = jnp.arange(owner_count, dtype=jnp.int32)
    counts = jnp.sum((owner_of[:, None] == owner_ids[None, :]).astype(jnp.int32), axis=0)
    starts = jnp.cumsum(counts) - counts
    slot_index = jnp.arange(capacity, dtype=jnp.int32)
    usable = slot_index[None, :] < counts[:, None]
    total_rows = owner_count * capacity
    token_index = jnp.arange(token_count, dtype=jnp.int32)
    wanted = jnp.where(usable, starts[:, None] + slot_index[None, :], -1).reshape(total_rows)
    pick = (wanted[:, None] == token_index[None, :]).astype(jnp.bfloat16)
    id_width = 128
    table = jnp.concatenate(
        [
            hidden,
            cotangent,
            jnp.broadcast_to(
                (region_ids % local_count + 1).astype(jnp.bfloat16)[:, None],
                (token_count, id_width),
            ),
        ],
        axis=-1,
    )
    send = jnp.dot(pick, table, preferred_element_type=jnp.float32).astype(jnp.bfloat16)
    send = send.reshape(owner_count, capacity, hidden_width + model_width + id_width)
    recv = lax.all_to_all(send, "dp", split_axis=0, concat_axis=0, tiled=True)
    recv = recv.reshape(total_rows, hidden_width + model_width + id_width)
    got_hidden = recv[:, :hidden_width]
    got_cotangent = recv[:, hidden_width : hidden_width + model_width]
    got_local = recv[:, hidden_width + model_width] - 1
    local_ids = jnp.arange(local_count).astype(jnp.bfloat16)
    onehot = (got_local[:, None] == local_ids[None, :]).astype(jnp.float32)
    flat_a = adapter_a.reshape(local_count * rank_width, hidden_width)
    flat_b = adapter_b.reshape(local_count * rank_width, model_width)
    part_down = contract_cols(got_hidden, flat_a).reshape(total_rows, local_count, rank_width)
    part_back = contract_cols(got_cotangent, flat_b).reshape(total_rows, local_count, rank_width)
    pick_down = jnp.sum(part_down * onehot[:, :, None], axis=1)
    pick_back = jnp.sum(part_back * onehot[:, :, None], axis=1)
    full = fsdp_sum(jnp.concatenate([pick_down, pick_back], axis=1))
    full_down = full[:, :rank_width].astype(jnp.bfloat16)
    full_back = full[:, rank_width:].astype(jnp.bfloat16)
    mask = onehot.astype(jnp.bfloat16)[:, :, None]
    down_rows = (mask * full_down[:, None, :]).reshape(total_rows, local_count * rank_width)
    back_rows = (mask * full_back[:, None, :]).reshape(total_rows, local_count * rank_width)
    grad_b = (
        contract_rows(down_rows, got_cotangent)
        .reshape(local_count, rank_width, model_width)
        .astype(jnp.bfloat16)
    )
    grad_a = (
        contract_rows(back_rows, got_hidden)
        .reshape(local_count, rank_width, hidden_width)
        .astype(jnp.bfloat16)
    )
    returned = jnp.dot(back_rows, flat_a, preferred_element_type=jnp.float32).astype(jnp.bfloat16)
    returned = returned.reshape(owner_count, capacity, hidden_width)
    arrived = lax.all_to_all(returned, "dp", split_axis=0, concat_axis=0, tiled=True)
    before = jnp.sum((owner_of[None, :] < owner_of[:, None]).astype(jnp.int32), axis=1)
    source = owner_of * capacity + token_index - before
    slot_all = jnp.arange(total_rows, dtype=jnp.int32)
    place = (source[:, None] == slot_all[None, :]).astype(jnp.bfloat16)
    grad_hidden = jnp.dot(
        place, arrived.reshape(total_rows, hidden_width), preferred_element_type=jnp.float32
    ).astype(jnp.bfloat16)
    return (grad_a, grad_b, grad_hidden)


def solution(mesh):
    return jax.shard_map(
        shards,
        mesh=mesh,
        in_specs=(
            P("dp", "fsdp"),
            P("dp", "fsdp"),
            P("dp"),
            P("dp", None, "fsdp"),
            P("dp", None, "fsdp"),
        ),
        out_specs=(P("dp", None, "fsdp"), P("dp", None, "fsdp"), P("dp", "fsdp")),
        check_vma=False,
    )
```

```python
import jax
import jax.numpy as jnp
from jax import lax
from jax.sharding import PartitionSpec as P


def contract_rows(left, right):
    return lax.dot_general(
        left, right, (((0,), (0,)), ((), ())), preferred_element_type=jnp.float32
    )


def contract_cols(left, right):
    return lax.dot_general(
        left, right, (((1,), (1,)), ((), ())), preferred_element_type=jnp.float32
    )


def fsdp_sum(x):
    n = lax.axis_size("fsdp")
    if n & (n - 1):
        return lax.psum(x, "fsdp")
    step = 1
    while step < n:
        x = x + lax.ppermute(x, "fsdp", [(i, i ^ step) for i in range(n)])
        step *= 2
    return x


def shards(hidden, cotangent, region_ids, adapter_a, adapter_b):
    owner_count = lax.axis_size("dp")
    token_count = hidden.shape[0]
    local_count = adapter_a.shape[0]
    rank_width = adapter_a.shape[1]
    hidden_width = hidden.shape[1]
    model_width = cotangent.shape[1]
    capacity = 3 * token_count // owner_count
    owner_of = region_ids // local_count
    owner_ids = jnp.arange(owner_count, dtype=jnp.int32)
    counts = jnp.sum((owner_of[:, None] == owner_ids[None, :]).astype(jnp.int32), axis=0)
    starts = jnp.cumsum(counts) - counts
    slot_index = jnp.arange(capacity, dtype=jnp.int32)
    usable = slot_index[None, :] < counts[:, None]
    total_rows = owner_count * capacity
    token_index = jnp.arange(token_count, dtype=jnp.int32)
    wanted = jnp.where(usable, starts[:, None] + slot_index[None, :], -1).reshape(total_rows)
    pick = (wanted[:, None] == token_index[None, :]).astype(jnp.bfloat16)
    id_width = 128
    table = jnp.concatenate(
        [
            hidden,
            cotangent,
            jnp.broadcast_to(
                (region_ids % local_count + 1).astype(jnp.bfloat16)[:, None],
                (token_count, id_width),
            ),
        ],
        axis=-1,
    )
    send = jnp.dot(pick, table, preferred_element_type=jnp.float32).astype(jnp.bfloat16)
    send = send.reshape(owner_count, capacity, hidden_width + model_width + id_width)
    recv = lax.all_to_all(send, "dp", split_axis=0, concat_axis=0, tiled=True)
    recv = recv.reshape(total_rows, hidden_width + model_width + id_width)
    got_hidden = recv[:, :hidden_width]
    got_cotangent = recv[:, hidden_width : hidden_width + model_width]
    got_local = recv[:, hidden_width + model_width] - 1
    local_ids = jnp.arange(local_count).astype(jnp.bfloat16)
    onehot = (got_local[:, None] == local_ids[None, :]).astype(jnp.float32)
    flat_a = adapter_a.reshape(local_count * rank_width, hidden_width)
    flat_b = adapter_b.reshape(local_count * rank_width, model_width)
    part_down = contract_cols(got_hidden, flat_a).reshape(total_rows, local_count, rank_width)
    part_back = contract_cols(got_cotangent, flat_b).reshape(total_rows, local_count, rank_width)
    pick_down = jnp.sum(part_down * onehot[:, :, None], axis=1)
    pick_back = jnp.sum(part_back * onehot[:, :, None], axis=1)
    full_back = fsdp_sum(pick_back).astype(jnp.bfloat16)
    full_down = fsdp_sum(pick_down).astype(jnp.bfloat16)
    mask = onehot.astype(jnp.bfloat16)[:, :, None]
    down_rows = (mask * full_down[:, None, :]).reshape(total_rows, local_count * rank_width)
    back_rows = (mask * full_back[:, None, :]).reshape(total_rows, local_count * rank_width)
    grad_b = (
        contract_rows(down_rows, got_cotangent)
        .reshape(local_count, rank_width, model_width)
        .astype(jnp.bfloat16)
    )
    grad_a = (
        contract_rows(back_rows, got_hidden)
        .reshape(local_count, rank_width, hidden_width)
        .astype(jnp.bfloat16)
    )
    returned = jnp.dot(back_rows, flat_a, preferred_element_type=jnp.float32).astype(jnp.bfloat16)
    returned = returned.reshape(owner_count, capacity, hidden_width)
    arrived = lax.all_to_all(returned, "dp", split_axis=0, concat_axis=0, tiled=True)
    before = jnp.sum((owner_of[None, :] < owner_of[:, None]).astype(jnp.int32), axis=1)
    source = owner_of * capacity + token_index - before
    slot_all = jnp.arange(total_rows, dtype=jnp.int32)
    place = (source[:, None] == slot_all[None, :]).astype(jnp.bfloat16)
    grad_hidden = jnp.dot(
        place, arrived.reshape(total_rows, hidden_width), preferred_element_type=jnp.float32
    ).astype(jnp.bfloat16)
    return (grad_a, grad_b, grad_hidden)


def solution(mesh):
    return jax.shard_map(
        shards,
        mesh=mesh,
        in_specs=(
            P("dp", "fsdp"),
            P("dp", "fsdp"),
            P("dp"),
            P("dp", None, "fsdp"),
            P("dp", None, "fsdp"),
        ),
        out_specs=(P("dp", None, "fsdp"), P("dp", None, "fsdp"), P("dp", "fsdp")),
        check_vma=False,
    )
```

```python
import jax
import jax.numpy as jnp
from jax import lax
from jax.sharding import PartitionSpec as P


def contract_rows(left, right):
    return lax.dot_general(
        left, right, (((0,), (0,)), ((), ())), preferred_element_type=jnp.float32
    )


def contract_cols(left, right):
    return lax.dot_general(
        left, right, (((1,), (1,)), ((), ())), preferred_element_type=jnp.float32
    )


def fsdp_sum(x):
    n = lax.axis_size("fsdp")
    if n & (n - 1):
        return lax.psum(x, "fsdp")
    step = 1
    while step < n:
        x = x + lax.ppermute(x, "fsdp", [(i, i ^ step) for i in range(n)])
        step *= 2
    return x


def shards(hidden, cotangent, region_ids, adapter_a, adapter_b):
    owner_count = lax.axis_size("dp")
    token_count = hidden.shape[0]
    local_count = adapter_a.shape[0]
    rank_width = adapter_a.shape[1]
    hidden_width = hidden.shape[1]
    model_width = cotangent.shape[1]
    capacity = 3 * token_count // owner_count
    owner_of = region_ids // local_count
    owner_ids = jnp.arange(owner_count, dtype=jnp.int32)
    counts = jnp.sum((owner_of[:, None] == owner_ids[None, :]).astype(jnp.int32), axis=0)
    starts = jnp.cumsum(counts) - counts
    slot_index = jnp.arange(capacity, dtype=jnp.int32)
    usable = slot_index[None, :] < counts[:, None]
    total_rows = owner_count * capacity
    token_index = jnp.arange(token_count, dtype=jnp.int32)
    wanted = jnp.where(usable, starts[:, None] + slot_index[None, :], -1).reshape(total_rows)
    pick = (wanted[:, None] == token_index[None, :]).astype(jnp.bfloat16)
    id_width = 128
    small = jnp.concatenate(
        [
            cotangent,
            jnp.broadcast_to(
                (region_ids % local_count + 1).astype(jnp.bfloat16)[:, None],
                (token_count, id_width),
            ),
        ],
        axis=-1,
    )
    send_small = jnp.dot(pick, small, preferred_element_type=jnp.float32).astype(jnp.bfloat16)
    send_small = send_small.reshape(owner_count, capacity, model_width + id_width)
    recv_small = lax.all_to_all(send_small, "dp", split_axis=0, concat_axis=0, tiled=True)
    recv_small = recv_small.reshape(total_rows, model_width + id_width)
    send_hidden = jnp.dot(pick, hidden, preferred_element_type=jnp.float32).astype(jnp.bfloat16)
    send_hidden = send_hidden.reshape(owner_count, capacity, hidden_width)
    got_hidden = lax.all_to_all(send_hidden, "dp", split_axis=0, concat_axis=0, tiled=True)
    got_hidden = got_hidden.reshape(total_rows, hidden_width)
    got_cotangent = recv_small[:, :model_width]
    got_local = recv_small[:, model_width] - 1
    local_ids = jnp.arange(local_count).astype(jnp.bfloat16)
    onehot = (got_local[:, None] == local_ids[None, :]).astype(jnp.float32)
    flat_a = adapter_a.reshape(local_count * rank_width, hidden_width)
    flat_b = adapter_b.reshape(local_count * rank_width, model_width)
    part_down = contract_cols(got_hidden, flat_a).reshape(total_rows, local_count, rank_width)
    part_back = contract_cols(got_cotangent, flat_b).reshape(total_rows, local_count, rank_width)
    pick_down = jnp.sum(part_down * onehot[:, :, None], axis=1)
    pick_back = jnp.sum(part_back * onehot[:, :, None], axis=1)
    full_back = fsdp_sum(pick_back).astype(jnp.bfloat16)
    full_down = fsdp_sum(pick_down).astype(jnp.bfloat16)
    mask = onehot.astype(jnp.bfloat16)[:, :, None]
    down_rows = (mask * full_down[:, None, :]).reshape(total_rows, local_count * rank_width)
    back_rows = (mask * full_back[:, None, :]).reshape(total_rows, local_count * rank_width)
    grad_b = (
        contract_rows(down_rows, got_cotangent)
        .reshape(local_count, rank_width, model_width)
        .astype(jnp.bfloat16)
    )
    grad_a = (
        contract_rows(back_rows, got_hidden)
        .reshape(local_count, rank_width, hidden_width)
        .astype(jnp.bfloat16)
    )
    returned = jnp.dot(back_rows, flat_a, preferred_element_type=jnp.float32).astype(jnp.bfloat16)
    returned = returned.reshape(owner_count, capacity, hidden_width)
    arrived = lax.all_to_all(returned, "dp", split_axis=0, concat_axis=0, tiled=True)
    before = jnp.sum((owner_of[None, :] < owner_of[:, None]).astype(jnp.int32), axis=1)
    source = owner_of * capacity + token_index - before
    slot_all = jnp.arange(total_rows, dtype=jnp.int32)
    place = (source[:, None] == slot_all[None, :]).astype(jnp.bfloat16)
    grad_hidden = jnp.dot(
        place, arrived.reshape(total_rows, hidden_width), preferred_element_type=jnp.float32
    ).astype(jnp.bfloat16)
    return (grad_a, grad_b, grad_hidden)


def solution(mesh):
    return jax.shard_map(
        shards,
        mesh=mesh,
        in_specs=(
            P("dp", "fsdp"),
            P("dp", "fsdp"),
            P("dp"),
            P("dp", None, "fsdp"),
            P("dp", None, "fsdp"),
        ),
        out_specs=(P("dp", None, "fsdp"), P("dp", None, "fsdp"), P("dp", "fsdp")),
        check_vma=False,
    )
```

```python
import jax
import jax.numpy as jnp
from jax import lax
from jax.sharding import PartitionSpec as P


def exchange(x):
    n = lax.axis_size("dp")
    me = lax.axis_index("dp")
    out = lax.dynamic_update_slice_in_dim(
        jnp.zeros_like(x), lax.dynamic_slice_in_dim(x, me, 1, 0), me, 0
    )
    for k in range(1, n):
        piece = lax.dynamic_slice_in_dim(x, (me + k) % n, 1, 0)
        got = lax.ppermute(piece, "dp", [(i, (i + k) % n) for i in range(n)])
        out = lax.dynamic_update_slice_in_dim(out, got, (me - k + n) % n, 0)
    return out


def contract_rows(left, right):
    return lax.dot_general(
        left, right, (((0,), (0,)), ((), ())), preferred_element_type=jnp.float32
    )


def contract_cols(left, right):
    return lax.dot_general(
        left, right, (((1,), (1,)), ((), ())), preferred_element_type=jnp.float32
    )


def fsdp_sum(x):
    n = lax.axis_size("fsdp")
    if n & (n - 1):
        return lax.psum(x, "fsdp")
    step = 1
    while step < n:
        x = x + lax.ppermute(x, "fsdp", [(i, i ^ step) for i in range(n)])
        step *= 2
    return x


def shards(hidden, cotangent, region_ids, adapter_a, adapter_b):
    owner_count = lax.axis_size("dp")
    token_count = hidden.shape[0]
    local_count = adapter_a.shape[0]
    rank_width = adapter_a.shape[1]
    hidden_width = hidden.shape[1]
    model_width = cotangent.shape[1]
    capacity = 3 * token_count // owner_count
    owner_of = region_ids // local_count
    owner_ids = jnp.arange(owner_count, dtype=jnp.int32)
    counts = jnp.sum((owner_of[:, None] == owner_ids[None, :]).astype(jnp.int32), axis=0)
    starts = jnp.cumsum(counts) - counts
    slot_index = jnp.arange(capacity, dtype=jnp.int32)
    usable = slot_index[None, :] < counts[:, None]
    total_rows = owner_count * capacity
    token_index = jnp.arange(token_count, dtype=jnp.int32)
    wanted = jnp.where(usable, starts[:, None] + slot_index[None, :], -1).reshape(total_rows)
    pick = (wanted[:, None] == token_index[None, :]).astype(jnp.bfloat16)
    id_width = 128
    small = jnp.concatenate(
        [
            cotangent,
            jnp.broadcast_to(
                (region_ids % local_count + 1).astype(jnp.bfloat16)[:, None],
                (token_count, id_width),
            ),
        ],
        axis=-1,
    )
    send_small = jnp.dot(pick, small, preferred_element_type=jnp.float32).astype(jnp.bfloat16)
    send_small = send_small.reshape(owner_count, capacity, model_width + id_width)
    recv_small = lax.all_to_all(send_small, "dp", split_axis=0, concat_axis=0, tiled=True)
    recv_small = recv_small.reshape(total_rows, model_width + id_width)
    send_hidden = jnp.dot(pick, hidden, preferred_element_type=jnp.float32).astype(jnp.bfloat16)
    send_hidden = send_hidden.reshape(owner_count, capacity, hidden_width)
    got_hidden = lax.all_to_all(send_hidden, "dp", split_axis=0, concat_axis=0, tiled=True)
    got_hidden = got_hidden.reshape(total_rows, hidden_width)
    got_cotangent = recv_small[:, :model_width]
    got_local = recv_small[:, model_width] - 1
    local_ids = jnp.arange(local_count).astype(jnp.bfloat16)
    onehot = (got_local[:, None] == local_ids[None, :]).astype(jnp.float32)
    flat_a = adapter_a.reshape(local_count * rank_width, hidden_width)
    flat_b = adapter_b.reshape(local_count * rank_width, model_width)
    part_down = contract_cols(got_hidden, flat_a).reshape(total_rows, local_count, rank_width)
    part_back = contract_cols(got_cotangent, flat_b).reshape(total_rows, local_count, rank_width)
    pick_down = jnp.sum(part_down * onehot[:, :, None], axis=1)
    pick_back = jnp.sum(part_back * onehot[:, :, None], axis=1)
    full_back = fsdp_sum(pick_back).astype(jnp.bfloat16)
    full_down = fsdp_sum(pick_down).astype(jnp.bfloat16)
    mask = onehot.astype(jnp.bfloat16)[:, :, None]
    down_rows = (mask * full_down[:, None, :]).reshape(total_rows, local_count * rank_width)
    back_rows = (mask * full_back[:, None, :]).reshape(total_rows, local_count * rank_width)
    grad_b = (
        contract_rows(down_rows, got_cotangent)
        .reshape(local_count, rank_width, model_width)
        .astype(jnp.bfloat16)
    )
    grad_a = (
        contract_rows(back_rows, got_hidden)
        .reshape(local_count, rank_width, hidden_width)
        .astype(jnp.bfloat16)
    )
    returned = jnp.dot(back_rows, flat_a, preferred_element_type=jnp.float32).astype(jnp.bfloat16)
    returned = returned.reshape(owner_count, capacity, hidden_width)
    arrived = exchange(returned)
    before = jnp.sum((owner_of[None, :] < owner_of[:, None]).astype(jnp.int32), axis=1)
    source = owner_of * capacity + token_index - before
    slot_all = jnp.arange(total_rows, dtype=jnp.int32)
    place = (source[:, None] == slot_all[None, :]).astype(jnp.bfloat16)
    grad_hidden = jnp.dot(
        place, arrived.reshape(total_rows, hidden_width), preferred_element_type=jnp.float32
    ).astype(jnp.bfloat16)
    return (grad_a, grad_b, grad_hidden)


def solution(mesh):
    return jax.shard_map(
        shards,
        mesh=mesh,
        in_specs=(
            P("dp", "fsdp"),
            P("dp", "fsdp"),
            P("dp"),
            P("dp", None, "fsdp"),
            P("dp", None, "fsdp"),
        ),
        out_specs=(P("dp", None, "fsdp"), P("dp", None, "fsdp"), P("dp", "fsdp")),
        check_vma=False,
    )
```
